32 devices in a mesh: scen: 4 (over y, x), col: 8 (over z, core).
Axes of the slice: x: 2, y: 2, z: 4, core: 2. Of those that a mesh axis runs over, the one named last changes fastest.
Arguments:
- border: float32 [8, 2048, 16384], P('scen', None, 'col'), may hold values from -0.046875 to 0.046875
- pattern: int32 [8, 16, 128], P('scen', None, 'col'), may hold values 0 or 1
- slack: float32 [8, 2048], P('scen'), may hold values from 0.5 to 2
- first_diag: float32 [16384], P('col'), may hold values from 0.25 to 1.75
- rhs: float32 [16384, 256], P('col'), may hold values from -6 to 6
- scen_rhs: float32 [8, 2048, 256], P('scen', 'col'), may hold values from -6 to 6
Outputs:
- reduced: float32 [8, 2048, 256], P('col', 'scen')
- directions: float32 [8, 2048, 256], P('scen', 'col')
The draws below stay inside these ranges and needn't reach their ends.
All inputs are finite; a program needn't handle non-finite values. No bound on the sum of `pattern` on one device may be relied on, other than what follows from the above.
Results may differ from the reference program's by a relative error of at most 0.0001.
Values sent between devices are 32-bit elements; how exact they have to be, the bound alone decides.
A program may use at most 192 MiB of HBM per device.

```python
import math
import jax
import jax.numpy as jnp
from jax import lax

N0 = 16384
PW = 512
NRHS = 256
ROWS = 2048
ROW_BLOCK = 128
COL_BLOCK = 128
SCEN_ALL = 8
FS_DEV = 2048
N_COL = 8


def draw_border(key, part):
    key_parts = jax.random.split(jax.random.fold_in(key, 7), 3)
    entry_scale = 1.0 / math.sqrt(SCEN_ALL * ROWS)
    separate = jax.random.normal(key_parts[0], (SCEN_ALL, ROWS, N0), jnp.float32)
    common_share = 0.2
    shared_rows = jax.random.normal(key_parts[1], (SCEN_ALL, ROWS, 1), jnp.float32)
    loading = jax.random.uniform(key_parts[2], (1, 1, N0), jnp.float32, 0.6, 1.4)
    mixture = math.sqrt(common_share) * shared_rows * loading + math.sqrt(1.0 - common_share) * separate
    limit_value = 5.9 * entry_scale
    return jnp.clip(entry_scale * mixture, -limit_value, limit_value).astype(jnp.float32)


def set_ends(entries, key, least, top_value):
    shape = entries.shape
    spot = [jax.random.randint(jax.random.fold_in(key, axis), (), 0, shape[axis]) for axis in range(len(shape))]
    entries = entries.at[tuple(spot)].set(least)
    longest = shape.index(max(shape))
    spot[longest] = (spot[longest] + 1) % shape[longest]
    return entries.at[tuple(spot)].set(top_value)


def steps_of(rng, extent, shards, low, largest):
    def one(position, blocks):
        draws = jax.random.uniform(jax.random.fold_in(jax.random.fold_in(rng, 6), position), (blocks,), jnp.float32, low / len(shards), largest / len(shards))
        return jnp.repeat(jnp.exp(draws), extent[position] // blocks).reshape((-1,) + (1,) * (len(extent) - position - 1))

    gain = one(*shards[0])
    for cut in shards[1:]:
        gain = gain * one(*cut)
    return gain


def gaussian(stream_key, extent, spread, reach, cuts=(), kind=jnp.bfloat16):
    array = jax.random.normal(stream_key, extent, jnp.float32) * spread
    if len(cuts) > 0:
        array = steps_of(stream_key, extent, cuts, -0.22, 0.18) * array
    return jnp.clip(array, min=-reach, max=reach).astype(kind)


def setup_inputs(seed: int = 0) -> dict:
    arg_keys = jax.random.split(jax.random.key(seed), 7)
    return {
        "border": draw_border(jax.random.fold_in(arg_keys[6], 71), 0),
        "pattern": set_ends((jax.random.randint(arg_keys[1], (SCEN_ALL, ROWS // ROW_BLOCK, N0 // COL_BLOCK), 0, 4) < 3).astype(jnp.int32), jax.random.fold_in(arg_keys[1], 1), 0, 1),
        "slack": jnp.clip(jnp.exp(math.log(2.0) - 1.3862944 * jax.random.uniform(arg_keys[2], (SCEN_ALL, ROWS), jnp.float32) ** steps_of(arg_keys[2], (SCEN_ALL, ROWS), ((0, 4),), -0.2, 0.2)), 0.5, 2.0),
        "first_diag": jnp.clip(1.0 + 0.15 * jax.random.normal(arg_keys[3], (N0,), jnp.float32), 0.25, 1.75),
        "rhs": gaussian(arg_keys[4], (N0, NRHS), 1.0, 6.0, ((0, 8),), jnp.float32),
        "scen_rhs": gaussian(arg_keys[5], (SCEN_ALL, ROWS, NRHS), 1.0, 6.0, ((0, 4), (1, 8)), jnp.float32),
    }


def expand(block_mask):
    ones = jnp.repeat(block_mask.astype(jnp.float32), ROW_BLOCK, axis=0)
    return jnp.repeat(ones, COL_BLOCK, axis=1)

def panel_index():
    order = jnp.arange(PW, dtype=jnp.int32)
    width_each = PW // N_COL
    return (order // width_each * (N0 // N_COL) + order % width_each).astype(jnp.int32)

def reference(border, pattern, slack, first_diag, rhs, scen_rhs):
    chosen = panel_index()
    order = jnp.arange(PW, dtype=jnp.int32)

    def accumulate(running, members):
        block_rows, block_mask, barrier = members
        masked = block_rows * expand(block_mask)
        panel_part = masked[:, chosen] / barrier[:, None]
        added = jnp.dot(masked.T.astype(jnp.float32), panel_part.astype(jnp.float32), precision=lax.Precision.HIGHEST, preferred_element_type=jnp.float32)
        return (running + added, None)
    schur, _ = lax.scan(accumulate, jnp.zeros((N0, PW), jnp.float32), (border, pattern, slack))
    schur = schur.at[chosen, order].add(first_diag[chosen])
    factor = jnp.linalg.cholesky(schur[chosen])
    forward = lax.linalg.triangular_solve(factor, rhs[chosen], left_side=True, lower=True)
    solved = lax.linalg.triangular_solve(factor, forward, left_side=True, lower=True, transpose_a=True)
    reduced = rhs - jnp.dot(schur.astype(jnp.float32), solved.astype(jnp.float32), precision=lax.Precision.HIGHEST, preferred_element_type=jnp.float32)
    reduced = reduced.at[chosen].set(forward)

    def direction(members):
        block_rows, block_mask, barrier, second_rhs = members
        panel_part = (block_rows * expand(block_mask))[:, chosen]
        moved = jnp.dot(panel_part.astype(jnp.float32), solved.astype(jnp.float32), precision=lax.Precision.HIGHEST, preferred_element_type=jnp.float32)
        return (second_rhs - moved) / barrier[:, None]
    directions = lax.map(direction, (border, pattern, slack, scen_rhs))
    return (reduced.reshape(N0 // FS_DEV, FS_DEV, NRHS), directions)
```

```python
import functools

import jax
import jax.numpy as jnp
from jax import lax
from jax.experimental import pallas as pl
from jax.experimental.pallas import tpu as pltpu
from jax.sharding import PartitionSpec as P

PW = 512
BLK = 128
HIGHEST = lax.Precision.HIGHEST


def dot(a, b, contract=((1,), (0,))):
    return lax.dot_general(
        a, b, (contract, ((), ())), precision=HIGHEST, preferred_element_type=jnp.float32
    )


def invert_factor(block):
    groups = BLK // 8
    shape = (8, BLK)
    sub = lax.broadcasted_iota(jnp.int32, shape, 0)
    lane = lax.broadcasted_iota(jnp.int32, shape, 1)
    rows = [block[8 * i : 8 * i + 8, :] for i in range(groups)]
    inverse = [jnp.where(lane == sub + 8 * i, 1.0, 0.0).astype(jnp.float32) for i in range(groups)]
    for g in range(groups):
        columns = [
            {i: jnp.broadcast_to(rows[i][:, 8 * g + m : 8 * g + m + 1], shape) for i in range(g, groups)}
            for m in range(8)
        ]
        pivots = jnp.ones(shape, jnp.float32)
        for m in range(8):
            head = columns[m][g]
            pivot = jnp.broadcast_to(head[m : m + 1, :], shape)
            scale = 1.0 / pivot
            pivots = jnp.where(sub == m, pivot, pivots)
            row = jnp.broadcast_to(rows[g][m : m + 1, :], shape) * scale
            inverse_row = jnp.broadcast_to(inverse[g][m : m + 1, :], shape) * scale
            factors = [
                jnp.broadcast_to(head[later : later + 1, :], shape) * scale for later in range(m + 1, 8)
            ]
            for i in range(g, groups):
                column = columns[m][i]
                if i == g:
                    column = jnp.where(sub > m, column, 0.0)
                rows[i] = rows[i] - column * row
                inverse[i] = inverse[i] - column * inverse_row
                for later in range(m + 1, 8):
                    columns[later][i] = columns[later][i] - column * factors[later - m - 1]
        inverse[g] = inverse[g] * lax.rsqrt(pivots)
    return jnp.concatenate(inverse, axis=0)


def solve_kernel(packed, rhs, forward, solved, matrix, right, upper, inverses):
    steps = matrix.shape[0] // BLK
    matrix[...] = jnp.zeros_like(matrix)
    offset = 0
    for i in range(steps):
        width = matrix.shape[1] - i * BLK
        matrix[i * BLK : (i + 1) * BLK, i * BLK :] = packed[:, offset : offset + width]
        offset += width
    right[...] = rhs[...]
    solved[...] = jnp.zeros_like(solved)

    def eliminate(j, carry):
        here = pl.ds(pl.multiple_of(j * BLK, BLK), BLK)
        inverse = invert_factor(matrix[here, here])
        inverses[here, :] = inverse
        wide = dot(inverse, matrix[here, :])
        part = dot(inverse, right[here, :])
        cols = lax.broadcasted_iota(jnp.int32, wide.shape, 1)
        wide = jnp.where(cols >= (j + 1) * BLK, wide, 0.0)
        upper[here, :] = wide
        forward[here, :] = part
        matrix[...] -= dot(wide, wide, ((0,), (0,)))
        right[...] -= dot(wide, part, ((0,), (0,)))
        return carry

    lax.fori_loop(0, steps, eliminate, 0)

    def substitute(t, carry):
        here = pl.ds(pl.multiple_of((steps - 1 - t) * BLK, BLK), BLK)
        rest = forward[here, :] - dot(upper[here, :], solved[...])
        solved[here, :] = dot(inverses[here, :], rest, ((0,), (0,)))
        return carry

    lax.fori_loop(0, steps, substitute, 0)


def factor_and_solve(packed, rhs):
    size, width = rhs.shape
    out = jax.ShapeDtypeStruct((size, width), jnp.float32)
    return pl.pallas_call(
        solve_kernel,
        out_shape=(out, out),
        in_specs=[pl.BlockSpec(memory_space=pltpu.VMEM)] * 2,
        out_specs=[pl.BlockSpec(memory_space=pltpu.VMEM)] * 2,
        scratch_shapes=[
            pltpu.VMEM((size, size), jnp.float32),
            pltpu.VMEM((size, width), jnp.float32),
            pltpu.VMEM((size, size), jnp.float32),
            pltpu.VMEM((size, BLK), jnp.float32),
        ],
    )(packed, rhs)


def halves(x):
    high = x.astype(jnp.bfloat16)
    return high, (x - high.astype(jnp.float32)).astype(jnp.bfloat16)


def apply_kernel(row_block, border, mask, weights, out, total):
    step = pl.program_id(0) * pl.num_programs(1) + pl.program_id(1)
    last = pl.num_programs(0) * pl.num_programs(1) - 1

    @pl.when(step == 0)
    def _():
        total[...] = jnp.zeros_like(total)

    blocks = [
        border[0, r * row_block : (r + 1) * row_block, :] * mask[0, r] for r in range(mask.shape[1])
    ]
    high, low = halves(jnp.concatenate(blocks, axis=0) if len(blocks) > 1 else blocks[0])
    w_high, w_low = halves(weights[0, 0])
    count = w_high.shape[0]
    both = jnp.dot(
        jnp.concatenate([w_high, w_low], axis=0), high, preferred_element_type=jnp.float32
    )
    total[...] += both[:count] + both[count:] + jnp.dot(w_high, low, preferred_element_type=jnp.float32)

    @pl.when(step == last)
    def _():
        share = out.shape[2]
        for d in range(out.shape[0]):
            out[d] = total[:, d * share : (d + 1) * share]


def apply_border(border, mask, weights, parts):
    scen_local, row_total, own_width = border.shape
    col_count, _, rhs_count, row_share = weights.shape
    row_block = row_total // mask.shape[1]
    per_step = row_share // row_block
    return pl.pallas_call(
        functools.partial(apply_kernel, row_block),
        grid=(scen_local, col_count),
        in_specs=[
            pl.BlockSpec((1, row_share, own_width), lambda s, c: (s, c, 0)),
            pl.BlockSpec((1, per_step, 1, own_width), lambda s, c: (s, c, 0, 0)),
            pl.BlockSpec((1, 1, rhs_count, row_share), lambda s, c: (c, s, 0, 0)),
        ],
        out_specs=pl.BlockSpec((parts, rhs_count, own_width // parts), lambda s, c: (0, 0, 0)),
        out_shape=jax.ShapeDtypeStruct((parts, rhs_count, own_width // parts), jnp.float32),
        scratch_shapes=[pltpu.VMEM((rhs_count, own_width), jnp.float32)],
        compiler_params=pltpu.CompilerParams(vmem_limit_bytes=40 << 20),
    )(border, mask, weights)


def per_device(border, pattern, slack, first_diag, rhs, scen_rhs):
    col_count = lax.axis_size("col")
    scen_count = lax.axis_size("scen")
    col_index = lax.axis_index("col")
    scen_index = lax.axis_index("scen")
    scen_local, row_total, own_width = border.shape
    row_blocks, width_blocks = pattern.shape[1:]
    row_block = row_total // row_blocks
    col_block = own_width // width_blocks
    pivot_width = PW // col_count
    row_share = row_total // col_count
    own_share = own_width // scen_count

    rhs_panel = lax.all_gather(rhs[:pivot_width], "col", axis=0, tiled=True)
    weights = pattern.astype(jnp.float32)
    row_weights = jnp.repeat(weights, row_block, axis=1)
    panel_weights = jnp.repeat(row_weights[:, :, : -(-pivot_width // col_block)], col_block, axis=2)
    own_panel = border[:, :, :pivot_width] * panel_weights[:, :, :pivot_width]
    sent = own_panel.reshape(scen_local, col_count, row_share, pivot_width).transpose(1, 0, 3, 2)
    got = lax.all_to_all(sent, "col", split_axis=0, concat_axis=0, tiled=True)
    panel = got.transpose(1, 0, 2, 3).reshape(scen_local, PW, row_share)

    slack_rows = lax.dynamic_slice_in_dim(slack, col_index * row_share, row_share, 1)
    inverse_slack = 1.0 / slack_rows
    gram = lax.dot_general(
        panel * inverse_slack[:, None, :],
        panel,
        (((0, 2), (0, 2)), ((), ())),
        precision=HIGHEST,
        preferred_element_type=jnp.float32,
    )
    order = jnp.arange(PW, dtype=jnp.int32)
    mine = (order // pivot_width == col_index) & (scen_index == 0)
    diagonal = jnp.where(mine, jnp.tile(first_diag[:pivot_width], col_count), 0.0)
    gram = gram + jnp.where(order[:, None] == order[None, :], diagonal[:, None], 0.0)
    packed = jnp.concatenate(
        [gram[i * BLK : (i + 1) * BLK, i * BLK :] for i in range(PW // BLK)], axis=1
    )
    packed = lax.psum(packed, ("scen", "col"))
    forward, solved = factor_and_solve(packed, rhs_panel)

    moved = lax.dot_general(
        solved,
        panel,
        (((0,), (1,)), ((), ())),
        precision=HIGHEST,
        preferred_element_type=jnp.float32,
    ).transpose(1, 0, 2)
    scaled = moved * inverse_slack[:, None, :]
    everyone = lax.all_gather(scaled, "col", axis=0)
    mask = jnp.repeat(weights, col_block, axis=2)[:, :, None, :]
    terms = apply_border(border, mask, everyone, scen_count)
    summed = lax.psum_scatter(terms, "scen", scatter_dimension=0, tiled=True)[0]

    directions = (scen_rhs - moved.transpose(0, 2, 1)) / slack_rows[:, :, None]
    row_start = scen_index * own_share
    rhs_rows = lax.dynamic_slice_in_dim(rhs, row_start, own_share)
    reduced = rhs_rows - summed.T
    own_forward = lax.dynamic_slice_in_dim(forward, col_index * pivot_width, pivot_width)
    padded = jnp.pad(own_forward, ((0, own_width - pivot_width), (0, 0)))
    placed = lax.dynamic_slice_in_dim(padded, row_start, own_share)
    local_rows = row_start + jnp.arange(own_share, dtype=jnp.int32)
    reduced = jnp.where((local_rows < pivot_width)[:, None], placed, reduced)
    return reduced[None], directions


def solution(mesh):
    return jax.shard_map(
        per_device,
        mesh=mesh,
        in_specs=(
            P("scen", None, "col"),
            P("scen", None, "col"),
            P("scen", None),
            P("col"),
            P("col", None),
            P("scen", "col", None),
        ),
        out_specs=(P("col", "scen", None), P("scen", "col", None)),
        check_vma=False,
    )
```

```python
import functools

import jax
import jax.numpy as jnp
from jax import lax
from jax.experimental import pallas as pl
from jax.experimental.pallas import tpu as pltpu
from jax.sharding import PartitionSpec as P

PW = 512
BLK = 128
HIGHEST = lax.Precision.HIGHEST


def dot(a, b, contract=((1,), (0,))):
    return lax.dot_general(
        a, b, (contract, ((), ())), precision=HIGHEST, preferred_element_type=jnp.float32
    )


def invert_factor(block):
    groups = BLK // 8
    shape = (8, BLK)
    sub = lax.broadcasted_iota(jnp.int32, shape, 0)
    lane = lax.broadcasted_iota(jnp.int32, shape, 1)
    rows = [block[8 * i : 8 * i + 8, :] for i in range(groups)]
    inverse = [jnp.where(lane == sub + 8 * i, 1.0, 0.0).astype(jnp.float32) for i in range(groups)]
    for g in range(groups):
        columns = [
            {i: jnp.broadcast_to(rows[i][:, 8 * g + m : 8 * g + m + 1], shape) for i in range(g, groups)}
            for m in range(8)
        ]
        pivots = jnp.ones(shape, jnp.float32)
        for m in range(8):
            head = columns[m][g]
            pivot = jnp.broadcast_to(head[m : m + 1, :], shape)
            scale = 1.0 / pivot
            pivots = jnp.where(sub == m, pivot, pivots)
            row = jnp.broadcast_to(rows[g][m : m + 1, :], shape) * scale
            inverse_row = jnp.broadcast_to(inverse[g][m : m + 1, :], shape) * scale
            factors = [
                jnp.broadcast_to(head[later : later + 1, :], shape) * scale for later in range(m + 1, 8)
            ]
            for i in range(g, groups):
                column = columns[m][i]
                if i == g:
                    column = jnp.where(sub > m, column, 0.0)
                rows[i] = rows[i] - column * row
                inverse[i] = inverse[i] - column * inverse_row
                for later in range(m + 1, 8):
                    columns[later][i] = columns[later][i] - column * factors[later - m - 1]
        inverse[g] = inverse[g] * lax.rsqrt(pivots)
    return jnp.concatenate(inverse, axis=0)


def solve_kernel(packed, rhs, forward, solved, matrix, right, upper, inverses):
    steps = matrix.shape[0] // BLK
    matrix[...] = jnp.zeros_like(matrix)
    offset = 0
    for i in range(steps):
        width = matrix.shape[1] - i * BLK
        matrix[i * BLK : (i + 1) * BLK, i * BLK :] = packed[:, offset : offset + width]
        offset += width
    right[...] = rhs[...]
    solved[...] = jnp.zeros_like(solved)

    def eliminate(j, carry):
        here = pl.ds(pl.multiple_of(j * BLK, BLK), BLK)
        inverse = invert_factor(matrix[here, here])
        inverses[here, :] = inverse
        wide = dot(inverse, matrix[here, :])
        part = dot(inverse, right[here, :])
        cols = lax.broadcasted_iota(jnp.int32, wide.shape, 1)
        wide = jnp.where(cols >= (j + 1) * BLK, wide, 0.0)
        upper[here, :] = wide
        forward[here, :] = part
        matrix[...] -= dot(wide, wide, ((0,), (0,)))
        right[...] -= dot(wide, part, ((0,), (0,)))
        return carry

    lax.fori_loop(0, steps, eliminate, 0)

    def substitute(t, carry):
        here = pl.ds(pl.multiple_of((steps - 1 - t) * BLK, BLK), BLK)
        rest = forward[here, :] - dot(upper[here, :], solved[...])
        solved[here, :] = dot(inverses[here, :], rest, ((0,), (0,)))
        return carry

    lax.fori_loop(0, steps, substitute, 0)


def factor_and_solve(packed, rhs):
    size, width = rhs.shape
    out = jax.ShapeDtypeStruct((size, width), jnp.float32)
    return pl.pallas_call(
        solve_kernel,
        out_shape=(out, out),
        in_specs=[pl.BlockSpec(memory_space=pltpu.VMEM)] * 2,
        out_specs=[pl.BlockSpec(memory_space=pltpu.VMEM)] * 2,
        scratch_shapes=[
            pltpu.VMEM((size, size), jnp.float32),
            pltpu.VMEM((size, width), jnp.float32),
            pltpu.VMEM((size, size), jnp.float32),
            pltpu.VMEM((size, BLK), jnp.float32),
        ],
    )(packed, rhs)


def halves(x):
    high = x.astype(jnp.bfloat16)
    return high, (x - high.astype(jnp.float32)).astype(jnp.bfloat16)


def apply_kernel(row_block, border, mask, weights, *rest):
    before, (out, total) = rest[:-2], rest[-2:]
    step = pl.program_id(0)

    @pl.when(step == 0)
    def _():
        total[...] = jnp.zeros_like(total)

    blocks = [
        border[0, r * row_block : (r + 1) * row_block, :] * mask[0, r] for r in range(mask.shape[1])
    ]
    high, low = halves(jnp.concatenate(blocks, axis=0) if len(blocks) > 1 else blocks[0])
    w_high, w_low = halves(weights[0])
    count = w_high.shape[0]
    both = jnp.dot(
        jnp.concatenate([w_high, w_low], axis=0), high, preferred_element_type=jnp.float32
    )
    total[...] += both[:count] + both[count:] + jnp.dot(w_high, low, preferred_element_type=jnp.float32)

    @pl.when(step == pl.num_programs(0) - 1)
    def _():
        share = out.shape[2]
        for d in range(out.shape[0]):
            value = total[:, d * share : (d + 1) * share]
            out[d] = value + before[0][d] if before else value


def apply_border(border, mask, weights, scenario, parts, before):
    _, row_total, own_width = border.shape
    col_count, rhs_count, row_share = weights.shape
    row_block = row_total // mask.shape[1]
    per_step = row_share // row_block
    whole = (parts, rhs_count, own_width // parts)
    return pl.pallas_call(
        functools.partial(apply_kernel, row_block),
        grid=(col_count,),
        in_specs=[
            pl.BlockSpec((1, row_share, own_width), lambda c: (scenario, c, 0)),
            pl.BlockSpec((1, per_step, 1, own_width), lambda c: (scenario, c, 0, 0)),
            pl.BlockSpec((1, rhs_count, row_share), lambda c: (c, 0, 0)),
        ]
        + [pl.BlockSpec(whole, lambda c: (0, 0, 0)) for _ in before],
        out_specs=pl.BlockSpec(whole, lambda c: (0, 0, 0)),
        out_shape=jax.ShapeDtypeStruct(whole, jnp.float32),
        scratch_shapes=[pltpu.VMEM((rhs_count, own_width), jnp.float32)],
        compiler_params=pltpu.CompilerParams(vmem_limit_bytes=40 << 20),
        cost_estimate=pl.CostEstimate(
            flops=6 * row_total * own_width * rhs_count,
            bytes_accessed=4 * row_total * own_width,
            transcendentals=0,
        ),
    )(border, mask, weights, *before)


def per_device(border, pattern, slack, first_diag, rhs, scen_rhs):
    col_count = lax.axis_size("col")
    scen_count = lax.axis_size("scen")
    col_index = lax.axis_index("col")
    scen_index = lax.axis_index("scen")
    scen_local, row_total, own_width = border.shape
    row_blocks, width_blocks = pattern.shape[1:]
    row_block = row_total // row_blocks
    col_block = own_width // width_blocks
    pivot_width = PW // col_count
    row_share = row_total // col_count
    own_share = own_width // scen_count

    weights = pattern.astype(jnp.float32)
    row_weights = jnp.repeat(weights, row_block, axis=1)
    panel_weights = jnp.repeat(row_weights[:, :, : -(-pivot_width // col_block)], col_block, axis=2)
    own_panel = border[:, :, :pivot_width] * panel_weights[:, :, :pivot_width]
    sent = own_panel.reshape(scen_local, col_count, row_share, pivot_width).transpose(1, 0, 3, 2)
    got = lax.all_to_all(sent, "col", split_axis=0, concat_axis=0, tiled=True)
    panel = got.transpose(1, 0, 2, 3).reshape(scen_local, PW, row_share)

    slack_rows = lax.dynamic_slice_in_dim(slack, col_index * row_share, row_share, 1)
    inverse_slack = 1.0 / slack_rows
    gram = lax.dot_general(
        panel * inverse_slack[:, None, :],
        panel,
        (((0, 2), (0, 2)), ((), ())),
        precision=HIGHEST,
        preferred_element_type=jnp.float32,
    )
    order = jnp.arange(PW, dtype=jnp.int32)
    mine = (order // pivot_width == col_index) & (scen_index == 0)
    diagonal = jnp.where(mine, jnp.tile(first_diag[:pivot_width], col_count), 0.0)
    gram = gram + jnp.where(order[:, None] == order[None, :], diagonal[:, None], 0.0)
    packed = jnp.concatenate(
        [gram[i * BLK : (i + 1) * BLK, i * BLK :] for i in range(PW // BLK)], axis=1
    )
    piece = lax.psum_scatter(packed, "col", scatter_dimension=0, tiled=True)
    piece = lax.psum(piece, "scen")
    own_rhs = rhs[:pivot_width].reshape(piece.shape[0], -1)
    joined = lax.all_gather(jnp.concatenate([piece, own_rhs], axis=1), "col", axis=0, tiled=True)
    rhs_panel = joined[:, packed.shape[1] :].reshape(PW, rhs.shape[1])
    forward, solved = factor_and_solve(joined[:, : packed.shape[1]], rhs_panel)

    moved = lax.dot_general(
        solved,
        panel,
        (((0,), (1,)), ((), ())),
        precision=HIGHEST,
        preferred_element_type=jnp.float32,
    ).transpose(1, 0, 2)
    scaled = moved * inverse_slack[:, None, :]
    mask = jnp.repeat(weights, col_block, axis=2)[:, :, None, :]
    terms = ()
    for scenario in range(scen_local):
        everyone = lax.all_gather(scaled[scenario], "col", axis=0)
        terms = (apply_border(border, mask, everyone, scenario, scen_count, terms),)
    terms = terms[0]
    summed = lax.psum_scatter(terms, "scen", scatter_dimension=0, tiled=True)[0]

    directions = (scen_rhs - moved.transpose(0, 2, 1)) / slack_rows[:, :, None]
    row_start = scen_index * own_share
    rhs_rows = lax.dynamic_slice_in_dim(rhs, row_start, own_share)
    reduced = rhs_rows - summed.T
    own_forward = lax.dynamic_slice_in_dim(forward, col_index * pivot_width, pivot_width)
    padded = jnp.pad(own_forward, ((0, own_width - pivot_width), (0, 0)))
    placed = lax.dynamic_slice_in_dim(padded, row_start, own_share)
    local_rows = row_start + jnp.arange(own_share, dtype=jnp.int32)
    reduced = jnp.where((local_rows < pivot_width)[:, None], placed, reduced)
    return reduced[None], directions


def solution(mesh):
    return jax.shard_map(
        per_device,
        mesh=mesh,
        in_specs=(
            P("scen", None, "col"),
            P("scen", None, "col"),
            P("scen", None),
            P("col"),
            P("col", None),
            P("scen", "col", None),
        ),
        out_specs=(P("col", "scen", None), P("scen", "col", None)),
        check_vma=False,
    )
```

```python
import functools

import jax
import jax.numpy as jnp
from jax import lax
from jax.experimental import pallas as pl
from jax.experimental.pallas import tpu as pltpu
from jax.sharding import PartitionSpec as P

PW = 512
BLK = 128
HIGHEST = lax.Precision.HIGHEST


def dot(a, b, contract=((1,), (0,))):
    return lax.dot_general(
        a, b, (contract, ((), ())), precision=HIGHEST, preferred_element_type=jnp.float32
    )


def invert_factor(block):
    groups = BLK // 8
    shape = (8, BLK)
    sub = lax.broadcasted_iota(jnp.int32, shape, 0)
    lane = lax.broadcasted_iota(jnp.int32, shape, 1)
    rows = [block[8 * i : 8 * i + 8, :] for i in range(groups)]
    inverse = [jnp.where(lane == sub + 8 * i, 1.0, 0.0).astype(jnp.float32) for i in range(groups)]
    for g in range(groups):
        columns = [
            {i: jnp.broadcast_to(rows[i][:, 8 * g + m : 8 * g + m + 1], shape) for i in range(g, groups)}
            for m in range(8)
        ]
        pivots = jnp.ones(shape, jnp.float32)
        for m in range(8):
            head = columns[m][g]
            pivot = jnp.broadcast_to(head[m : m + 1, :], shape)
            scale = 1.0 / pivot
            pivots = jnp.where(sub == m, pivot, pivots)
            row = jnp.broadcast_to(rows[g][m : m + 1, :], shape) * scale
            inverse_row = jnp.broadcast_to(inverse[g][m : m + 1, :], shape) * scale
            factors = [
                jnp.broadcast_to(head[later : later + 1, :], shape) * scale for later in range(m + 1, 8)
            ]
            for i in range(g, groups):
                column = columns[m][i]
                if i == g:
                    column = jnp.where(sub > m, column, 0.0)
                rows[i] = rows[i] - column * row
                inverse[i] = inverse[i] - column * inverse_row
                for later in range(m + 1, 8):
                    columns[later][i] = columns[later][i] - column * factors[later - m - 1]
        inverse[g] = inverse[g] * lax.rsqrt(pivots)
    return jnp.concatenate(inverse, axis=0)


def solve_kernel(packed, rhs, forward, solved, matrix, right, upper, inverses):
    steps = matrix.shape[0] // BLK
    matrix[...] = jnp.zeros_like(matrix)
    offset = 0
    for i in range(steps):
        width = matrix.shape[1] - i * BLK
        matrix[i * BLK : (i + 1) * BLK, i * BLK :] = packed[:, offset : offset + width]
        offset += width
    right[...] = rhs[...]
    solved[...] = jnp.zeros_like(solved)

    def eliminate(j, carry):
        here = pl.ds(pl.multiple_of(j * BLK, BLK), BLK)
        inverse = invert_factor(matrix[here, here])
        inverses[here, :] = inverse
        wide = dot(inverse, matrix[here, :])
        part = dot(inverse, right[here, :])
        cols = lax.broadcasted_iota(jnp.int32, wide.shape, 1)
        wide = jnp.where(cols >= (j + 1) * BLK, wide, 0.0)
        upper[here, :] = wide
        forward[here, :] = part
        matrix[...] -= dot(wide, wide, ((0,), (0,)))
        right[...] -= dot(wide, part, ((0,), (0,)))
        return carry

    lax.fori_loop(0, steps, eliminate, 0)

    def substitute(t, carry):
        here = pl.ds(pl.multiple_of((steps - 1 - t) * BLK, BLK), BLK)
        rest = forward[here, :] - dot(upper[here, :], solved[...])
        solved[here, :] = dot(inverses[here, :], rest, ((0,), (0,)))
        return carry

    lax.fori_loop(0, steps, substitute, 0)


def factor_and_solve(packed, rhs):
    size, width = rhs.shape
    out = jax.ShapeDtypeStruct((size, width), jnp.float32)
    return pl.pallas_call(
        solve_kernel,
        out_shape=(out, out),
        in_specs=[pl.BlockSpec(memory_space=pltpu.VMEM)] * 2,
        out_specs=[pl.BlockSpec(memory_space=pltpu.VMEM)] * 2,
        scratch_shapes=[
            pltpu.VMEM((size, size), jnp.float32),
            pltpu.VMEM((size, width), jnp.float32),
            pltpu.VMEM((size, size), jnp.float32),
            pltpu.VMEM((size, BLK), jnp.float32),
        ],
    )(packed, rhs)


def halves(x):
    high = x.astype(jnp.bfloat16)
    return high, (x - high.astype(jnp.float32)).astype(jnp.bfloat16)


def apply_kernel(row_block, border, mask, weights, *rest):
    before, (out, total) = rest[:-2], rest[-2:]
    step = pl.program_id(0)

    @pl.when(step == 0)
    def _():
        total[...] = jnp.zeros_like(total)

    blocks = [
        border[0, r * row_block : (r + 1) * row_block, :] * mask[0, r] for r in range(mask.shape[1])
    ]
    high, low = halves(jnp.concatenate(blocks, axis=0) if len(blocks) > 1 else blocks[0])
    w_high, w_low = halves(weights[0])
    count = w_high.shape[0]
    both = jnp.dot(
        jnp.concatenate([w_high, w_low], axis=0), high, preferred_element_type=jnp.float32
    )
    total[...] += both[:count] + both[count:] + jnp.dot(w_high, low, preferred_element_type=jnp.float32)

    @pl.when(step == pl.num_programs(0) - 1)
    def _():
        share = out.shape[2]
        for d in range(out.shape[0]):
            value = total[:, d * share : (d + 1) * share]
            out[d] = value + before[0][d] if before else value


def apply_border(border, mask, weights, scenario, parts, before):
    _, row_total, own_width = border.shape
    col_count, rhs_count, row_share = weights.shape
    row_block = row_total // mask.shape[1]
    per_step = row_share // row_block
    whole = (parts, rhs_count, own_width // parts)
    return pl.pallas_call(
        functools.partial(apply_kernel, row_block),
        grid=(col_count,),
        in_specs=[
            pl.BlockSpec((1, row_share, own_width), lambda c: (scenario, c, 0)),
            pl.BlockSpec((1, per_step, 1, own_width), lambda c: (scenario, c, 0, 0)),
            pl.BlockSpec((1, rhs_count, row_share), lambda c: (c, 0, 0)),
        ]
        + [pl.BlockSpec(whole, lambda c: (0, 0, 0)) for _ in before],
        out_specs=pl.BlockSpec(whole, lambda c: (0, 0, 0)),
        out_shape=jax.ShapeDtypeStruct(whole, jnp.float32),
        scratch_shapes=[pltpu.VMEM((rhs_count, own_width), jnp.float32)],
        compiler_params=pltpu.CompilerParams(vmem_limit_bytes=40 << 20),
        cost_estimate=pl.CostEstimate(
            flops=6 * row_total * own_width * rhs_count,
            bytes_accessed=4 * row_total * own_width,
            transcendentals=0,
        ),
    )(border, mask, weights, *before)


def per_device(border, pattern, slack, first_diag, rhs, scen_rhs):
    col_count = lax.axis_size("col")
    scen_count = lax.axis_size("scen")
    col_index = lax.axis_index("col")
    scen_index = lax.axis_index("scen")
    scen_local, row_total, own_width = border.shape
    row_blocks, width_blocks = pattern.shape[1:]
    row_block = row_total // row_blocks
    col_block = own_width // width_blocks
    pivot_width = PW // col_count
    row_share = row_total // col_count
    own_share = own_width // scen_count

    weights = pattern.astype(jnp.float32)
    row_weights = jnp.repeat(weights, row_block, axis=1)
    panel_weights = jnp.repeat(row_weights[:, :, : -(-pivot_width // col_block)], col_block, axis=2)
    own_panel = border[:, :, :pivot_width] * panel_weights[:, :, :pivot_width]
    sent = own_panel.reshape(scen_local, col_count, row_share, pivot_width).transpose(1, 0, 3, 2)
    got = lax.all_to_all(sent, "col", split_axis=0, concat_axis=0, tiled=True)
    panel = got.transpose(1, 0, 2, 3).reshape(scen_local, PW, row_share)

    slack_rows = lax.dynamic_slice_in_dim(slack, col_index * row_share, row_share, 1)
    inverse_slack = 1.0 / slack_rows
    gram = lax.dot_general(
        panel * inverse_slack[:, None, :],
        panel,
        (((0, 2), (0, 2)), ((), ())),
        precision=HIGHEST,
        preferred_element_type=jnp.float32,
    )
    order = jnp.arange(PW, dtype=jnp.int32)
    mine = (order // pivot_width == col_index) & (scen_index == 0)
    diagonal = jnp.where(mine, jnp.tile(first_diag[:pivot_width], col_count), 0.0)
    gram = gram + jnp.where(order[:, None] == order[None, :], diagonal[:, None], 0.0)
    packed = jnp.concatenate(
        [gram[i * BLK : (i + 1) * BLK, i * BLK :] for i in range(PW // BLK)], axis=1
    )
    pieces = lax.all_to_all(
        packed.reshape(col_count, -1, packed.shape[1]), "col", split_axis=0, concat_axis=0, tiled=True
    )
    piece = lax.all_gather(jnp.sum(pieces, axis=0), "scen", axis=0).sum(axis=0)
    own_rhs = rhs[:pivot_width].reshape(piece.shape[0], -1)
    joined = lax.all_gather(jnp.concatenate([piece, own_rhs], axis=1), "col", axis=0, tiled=True)
    rhs_panel = joined[:, packed.shape[1] :].reshape(PW, rhs.shape[1])
    forward, solved = factor_and_solve(joined[:, : packed.shape[1]], rhs_panel)

    moved = lax.dot_general(
        solved,
        panel,
        (((0,), (1,)), ((), ())),
        precision=HIGHEST,
        preferred_element_type=jnp.float32,
    ).transpose(1, 0, 2)
    scaled = moved * inverse_slack[:, None, :]
    mask = jnp.repeat(weights, col_block, axis=2)[:, :, None, :]
    terms = ()
    for scenario in range(scen_local):
        everyone = lax.all_gather(scaled[scenario], "col", axis=0)
        terms = (apply_border(border, mask, everyone, scenario, scen_count, terms),)
    terms = terms[0]
    summed = lax.all_to_all(terms, "scen", split_axis=0, concat_axis=0, tiled=True).sum(axis=0)

    directions = (scen_rhs - moved.transpose(0, 2, 1)) / slack_rows[:, :, None]
    row_start = scen_index * own_share
    rhs_rows = lax.dynamic_slice_in_dim(rhs, row_start, own_share)
    reduced = rhs_rows - summed.T
    own_forward = lax.dynamic_slice_in_dim(forward, col_index * pivot_width, pivot_width)
    padded = jnp.pad(own_forward, ((0, own_width - pivot_width), (0, 0)))
    placed = lax.dynamic_slice_in_dim(padded, row_start, own_share)
    local_rows = row_start + jnp.arange(own_share, dtype=jnp.int32)
    reduced = jnp.where((local_rows < pivot_width)[:, None], placed, reduced)
    return reduced[None], directions


def solution(mesh):
    return jax.shard_map(
        per_device,
        mesh=mesh,
        in_specs=(
            P("scen", None, "col"),
            P("scen", None, "col"),
            P("scen", None),
            P("col"),
            P("col", None),
            P("scen", "col", None),
        ),
        out_specs=(P("col", "scen", None), P("scen", "col", None)),
        check_vma=False,
    )
```
